32 devices in a mesh: gx: 8 (over z, core), yz: 4 (over y, x).
Axes of the slice: x: 2, y: 2, z: 4, core: 2. Of those that a mesh axis runs over, the one named last changes fastest.
Arguments:
- leaf_moments: bfloat16 [64, 32, 256], P('gx', 'yz'), may hold values from -6 to 6
- leaf_list: int32 [64, 32, 16], P('gx', 'yz'), may hold values from 0 to 288
- leaf_op: int32 [64, 32, 16], P('gx', 'yz'), may hold values from 0 to 15
- leaf_parent: int32 [64, 32], P('gx', 'yz'), may hold values from 0 to 31, as said below
- leaf_octant: int32 [64, 32], P('gx', 'yz'), may hold values from 0 to 7, as said below
- parent_list: int32 [8, 32, 8], P('gx', 'yz'), may hold values from 0 to 159
- parent_op: int32 [8, 32, 8], P('gx', 'yz'), may hold values from 0 to 15
- operators: bfloat16 [16, 256, 256], replicated, may hold values from -0.09375 to 0.09375
- shift_up: bfloat16 [8, 256, 256], replicated, may hold values from -0.125 to 0.125
- density: bfloat16 [512, 128, 128], P(('gx', 'yz')), may hold values from -6 to 6
- nearby_coulomb_kernel: bfloat16 [8, 128, 128], replicated, may hold values from -0.1875 to 0.1875
- near_src: int32 [512, 16], P(('gx', 'yz')), may hold values from 0 to 15
- near_kind: int32 [512, 16], P(('gx', 'yz')), may hold values from 0 to 7
- near_count: int32 [512], P(('gx', 'yz')), may hold values from 1 to 16
- eval_rows: float32 [128, 16], replicated, may hold values from -1.5 to 1.5
- eval_cols: float32 [16, 128], replicated, may hold values from -1.5 to 1.5
Outputs:
- coulomb: bfloat16 [512, 128, 128], P(('gx', 'yz'))
The draws below stay inside these ranges and needn't reach their ends.
Inputs may be any that keep to these rules, and one draw needn't show every extreme that they name: `leaf_parent`: within each column of leaf blocks (a // 8 fixed) every coarse box number is named by exactly 8 leaves. `leaf_octant`: the 8 leaves of one coarse box have 8 different octants.
All inputs are finite; a program needn't handle non-finite values.
Results may differ from the reference program's by a relative error of at most 0.0026.
Values may be sent and summed in bfloat16 or wider, within the bound.
A program may use at most 64 MiB of HBM per device.

```python
import jax
import jax.numpy as jnp
from jax import lax

P_SIZE = 256
HARM = 16
SHELL = 128
LEAF_SIDE = 8
LIST = 16
PLIST = 8
OPS = 16
KINDS = 8
NEAR = 16
BOX_TILE = 4
GXB = 64
YZB = 32
PAR_COL = 32
TILES_DEV = 16
TILES = 512
N_GX = 8
N_YZ = 4


def family_codes(key):
    column_count = GXB // LEAF_SIDE
    keys = jax.random.split(jax.random.fold_in(key, 11), column_count)
    orders = jax.vmap(lambda one_key: jax.random.permutation(one_key, 8 * PAR_COL))(keys)
    return orders.reshape(GXB, YZB).astype(jnp.int32)


def draw_leaf_parent(key, part):
    return family_codes(key) // 8


def draw_leaf_octant(key, part):
    return family_codes(key) % 8


def draw_near_count(key, part):
    blocks_count = TILES // TILES_DEV
    limits = jax.random.randint(jax.random.fold_in(key, 1), (blocks_count,), NEAR // 4, NEAR + 1)
    picked = jax.random.randint(jax.random.fold_in(key, 2), (), 0, blocks_count)
    limits = jnp.where(jnp.arange(blocks_count) == picked, NEAR, limits)
    counts = jax.random.randint(jax.random.fold_in(key, 3), (blocks_count, TILES_DEV), 1, limits[:, None] + 1)
    counts = jnp.where(jnp.arange(TILES_DEV)[None, :] == 0, limits[:, None], counts)
    return counts.reshape(TILES).astype(jnp.int32)


def place_ends(result, rng, smallest, top_value):
    longest = result.shape.index(max(result.shape))
    spots = []
    for shift in (0, 1):
        where = [jax.random.randint(jax.random.fold_in(rng, axis), (), 0, length) for axis, length in enumerate(result.shape)]
        where[longest] = (where[longest] + shift) % result.shape[longest]
        spots.append(tuple(where))
    return result.at[spots[0]].set(smallest).at[spots[1]].set(top_value)


def shard_levels(rng, shape, shards, low, top_value):
    factor_of = 1.0
    for dim, parts in shards:
        heights = jax.random.uniform(jax.random.fold_in(jax.random.fold_in(rng, 6), dim), (parts,), jnp.float32, low / len(shards), top_value / len(shards))
        factor_of = factor_of * jnp.repeat(jnp.exp(heights), shape[dim] // parts).reshape((-1,) + (1,) * (len(shape) - 1 - dim))
    return factor_of


def bell_draw(key, dims, scale, reach, shards=(), kind=jnp.bfloat16):
    values = scale * jax.random.normal(key, dims, jnp.float32)
    if shards:
        values = values * shard_levels(key, dims, shards, -0.22, 0.18)
    return jnp.clip(values, -reach, reach).astype(kind)


def setup_inputs(seed: int = 0) -> dict:
    seeds = jax.random.split(jax.random.key(seed), 17)
    leaf_moments = bell_draw(seeds[0], (GXB, YZB, P_SIZE), 1.0, 6.0, ((0, 8), (1, 4)))
    leaf_list = place_ends(jax.random.randint(seeds[1], (GXB, YZB, LIST), 0, (2 * LEAF_SIDE + 1) * (2 * LEAF_SIDE + 1)), jax.random.fold_in(seeds[1], 1), 0, ((2 * LEAF_SIDE + 1) * (2 * LEAF_SIDE + 1)) - 1).astype(jnp.int32)
    leaf_op = place_ends(jax.random.randint(seeds[2], (GXB, YZB, LIST), 0, OPS), jax.random.fold_in(seeds[2], 1), 0, OPS - 1).astype(jnp.int32)
    leaf_parent = draw_leaf_parent(jax.random.fold_in(seeds[16], 71), 0)
    leaf_octant = draw_leaf_octant(jax.random.fold_in(seeds[16], 71), 0)
    parent_list = place_ends(jax.random.randint(seeds[5], (N_GX, PAR_COL, PLIST), 0, 5 * PAR_COL), jax.random.fold_in(seeds[5], 1), 0, (5 * PAR_COL) - 1).astype(jnp.int32)
    parent_op = place_ends(jax.random.randint(seeds[6], (N_GX, PAR_COL, PLIST), 0, OPS), jax.random.fold_in(seeds[6], 1), 0, OPS - 1).astype(jnp.int32)
    operators = bell_draw(seeds[7], (OPS, P_SIZE, P_SIZE), (P_SIZE * LIST) ** -0.5, 0.09375)
    shift_up = bell_draw(seeds[8], (8, P_SIZE, P_SIZE), (8 * P_SIZE) ** -0.5, 0.125)
    density = bell_draw(seeds[9], (TILES, SHELL, SHELL), 1.0, 6.0, ((0, 32),))
    nearby_coulomb_kernel = bell_draw(seeds[10], (KINDS, SHELL, SHELL), (SHELL * NEAR // 2) ** -0.5, 0.1875)
    near_src = place_ends(jax.random.randint(seeds[11], (TILES, NEAR), 0, TILES_DEV), jax.random.fold_in(seeds[11], 1), 0, TILES_DEV - 1).astype(jnp.int32)
    near_kind = place_ends(jax.random.randint(seeds[12], (TILES, NEAR), 0, KINDS), jax.random.fold_in(seeds[12], 1), 0, KINDS - 1).astype(jnp.int32)
    near_count = draw_near_count(jax.random.fold_in(seeds[16], 71), 0)
    eval_rows = bell_draw(seeds[14], (SHELL, HARM), HARM ** -0.5, 1.5, (), jnp.float32)
    eval_cols = bell_draw(seeds[15], (HARM, SHELL), HARM ** -0.5, 1.5, (), jnp.float32)
    return {"leaf_moments": leaf_moments, "leaf_list": leaf_list, "leaf_op": leaf_op, "leaf_parent": leaf_parent, "leaf_octant": leaf_octant, "parent_list": parent_list, "parent_op": parent_op, "operators": operators, "shift_up": shift_up, "density": density, "nearby_coulomb_kernel": nearby_coulomb_kernel, "near_src": near_src, "near_kind": near_kind, "near_count": near_count, "eval_rows": eval_rows, "eval_cols": eval_cols}


def grouped_products(sources, op_index, operators):
    summed = jnp.zeros(sources[0].shape, jnp.float32)
    for operator_number in range(operators.shape[0]):
        collected_tiles = jnp.zeros(sources[0].shape, jnp.float32)
        for slot_number in range(len(sources)):
            picked = (op_index[..., slot_number] == operator_number)[..., None]
            collected_tiles = collected_tiles + jnp.where(picked, sources[slot_number].astype(jnp.float32), jnp.float32(0.0))
        summed = summed + jnp.einsum("...p,pq->...q", collected_tiles, operators[operator_number].astype(jnp.float32), precision=lax.Precision.HIGHEST)
    return summed


def reference(leaf_moments, leaf_list, leaf_op, leaf_parent, leaf_octant, parent_list, parent_op, operators, shift_up, density, nearby_coulomb_kernel, near_src, near_kind, near_count, eval_rows, eval_cols):
    code_span = 2 * LEAF_SIDE + 1
    index_first = lax.broadcasted_iota(jnp.int32, (GXB, YZB), 0)
    index_second = lax.broadcasted_iota(jnp.int32, (GXB, YZB), 1)
    sources = []
    for slot_number in range(LIST):
        slot_code = leaf_list[:, :, slot_number]
        row_first = (index_first + slot_code // code_span - LEAF_SIDE) % GXB
        row_second = (index_second + slot_code % code_span - LEAF_SIDE) % YZB
        sources.append(leaf_moments[row_first, row_second])
    far_local = grouped_products(sources, leaf_op, operators)
    moments_wide = leaf_moments.astype(jnp.float32)
    translated = jnp.zeros((GXB, YZB, P_SIZE), jnp.float32)
    for octant in range(8):
        chosen = jnp.where((leaf_octant == octant)[..., None], moments_wide, jnp.float32(0.0))
        translated = translated + jnp.einsum("xyp,pq->xyq", chosen, shift_up[octant].astype(jnp.float32), precision=lax.Precision.HIGHEST)
    segment = (index_first // LEAF_SIDE) * PAR_COL + leaf_parent
    parent_moments = jax.ops.segment_sum(translated.reshape(GXB * YZB, P_SIZE), segment.reshape(GXB * YZB), num_segments=N_GX * PAR_COL)
    parent_moments = parent_moments.reshape(N_GX, PAR_COL, P_SIZE).astype(jnp.bfloat16)
    column_index = lax.broadcasted_iota(jnp.int32, (N_GX, PAR_COL), 0)
    coarse_sources = []
    for slot_number in range(PLIST):
        slot_code = parent_list[:, :, slot_number]
        source_column = (column_index + slot_code // PAR_COL - 2) % N_GX
        coarse_sources.append(parent_moments[source_column, slot_code % PAR_COL])
    parent_locals = grouped_products(coarse_sources, parent_op, operators).astype(jnp.bfloat16)
    parent_rows = parent_locals[index_first // LEAF_SIDE, leaf_parent].astype(jnp.float32)
    lowered = jnp.zeros((GXB, YZB, P_SIZE), jnp.float32)
    for octant in range(8):
        chosen = jnp.where((leaf_octant == octant)[..., None], parent_rows, jnp.float32(0.0))
        lowered = lowered + jnp.einsum("xyp,qp->xyq", chosen, shift_up[octant].astype(jnp.float32), precision=lax.Precision.HIGHEST)
    leaf_local = far_local + lowered
    blocks = leaf_local.reshape(N_GX, LEAF_SIDE, N_YZ, LEAF_SIDE, P_SIZE).transpose(0, 2, 1, 3, 4)
    blocks = blocks.reshape(TILES, BOX_TILE, HARM, HARM)
    left_half = jnp.einsum("rai,trij->traj", eval_rows.reshape(BOX_TILE, SHELL // BOX_TILE, HARM), blocks, precision=lax.Precision.HIGHEST)
    left_half = left_half.reshape(TILES, SHELL, HARM)
    far_tiles = jnp.einsum("taj,jb->tab", left_half, eval_cols, precision=lax.Precision.HIGHEST)
    tile_base = (jnp.arange(TILES, dtype=jnp.int32) // TILES_DEV) * TILES_DEV
    nearby_tile_list = jnp.zeros((TILES, SHELL, SHELL), jnp.float32)
    for interaction_kind in range(KINDS):
        collected_tiles = jnp.zeros((TILES, SHELL, SHELL), jnp.float32)
        for slot_number in range(NEAR):
            taken = (near_kind[:, slot_number] == interaction_kind) & (slot_number < near_count)
            paired_shell = density[tile_base + near_src[:, slot_number]].astype(jnp.float32)
            collected_tiles = collected_tiles + jnp.where(taken[:, None, None], paired_shell, jnp.float32(0.0))
        nearby_tile_list = nearby_tile_list + jnp.einsum("zf,pfo->pzo", nearby_coulomb_kernel[interaction_kind].astype(jnp.float32), collected_tiles, precision=lax.Precision.HIGHEST)
    return (nearby_tile_list + far_tiles).astype(jnp.bfloat16)
```

```python
import functools

import jax
import jax.numpy as jnp
from jax import lax
from jax.experimental import pallas as pl
from jax.experimental.pallas import tpu as pltpu
from jax.sharding import PartitionSpec as P

MESH = pl.DeviceIdType.MESH
F32 = jnp.float32
BF16 = jnp.bfloat16


def iota(shape, dim):
    return lax.broadcasted_iota(jnp.int32, shape, dim)


def dot(a, b):
    return jnp.dot(a, b, preferred_element_type=F32)


def split(value):
    high = value.astype(BF16)
    return high, (value - high.astype(F32)).astype(BF16)


def listed_sum(window_ref, codes, op_index, ops_ref, hot_ref, picked_ref, wide_ref, lhs_ref):
    rows, slots = codes.shape
    depth, coeffs = window_ref.shape
    ops_count = ops_ref.shape[0]
    places = iota((rows, depth), 1)
    for s in range(slots):
        hot_ref[s * rows : (s + 1) * rows, :] = jnp.where(
            codes[:, s : s + 1] == places, 1.0, 0.0
        ).astype(BF16)
    picked_ref[...] = dot(hot_ref[...], window_ref[...])
    for s in range(slots):
        wide_ref[s * rows : (s + 1) * rows, :] = jnp.broadcast_to(op_index[:, s : s + 1], (rows, 128))

    def collect(chunk, carry):
        base = pl.multiple_of(chunk * 16, 16)
        for half in range(coeffs // 128):
            lanes = slice(half * 128, (half + 1) * 128)
            for o in range(ops_count):
                total = jnp.zeros((16, 128), F32)
                for s in range(slots):
                    here = pl.ds(s * rows + base, 16)
                    total += jnp.where(wide_ref[here, :] == o, picked_ref[here, lanes], 0.0)
                high, low = split(total)
                at = o * coeffs + half * 128
                lhs_ref[pl.ds(base, 16), at : at + 128] = high
                lhs_ref[pl.ds(rows + base, 16), at : at + 128] = low
        return carry

    lax.fori_loop(0, rows // 16, collect, 0)
    both = dot(lhs_ref[...], ops_ref[...].reshape(ops_count * coeffs, coeffs))
    return both[:rows] + both[rows:]


def kernel(
    n_gx, n_yz, leaf_side,
    mom, llist, lop, lpar, loct, plist, pop, erows, ecols, nsrc, nkind, ncount,
    ops_hbm, shift_hbm, dens_hbm, kern_hbm,
    out,
    ops, shift, dens, kern,
    win, col_list, col_op, part, pwin,
    table, near, far, local,
    hot, picked, wide, lhs, hot2, picked2, wide2, lhs2,
    erep, cboth,
    load_sem, halo_send, halo_recv, list_send, list_recv, part_send, part_recv, par_send, par_recv,
):
    gx, yz = lax.axis_index("gx"), lax.axis_index("yz")
    leaves, coeffs = mom.shape
    kinds, shell = kern.shape[0], kern.shape[1]
    tiles = dens.shape[0]
    octants = shift.shape[0]
    column = part.shape[1]
    per_dev = plist.shape[0]
    harm = erows.shape[1]
    box_tile = leaves // tiles
    span = 2 * leaf_side + 1

    def at(dg, dy):
        return (lax.rem(gx + dg + 2 * n_gx, n_gx), lax.rem(yz + dy + n_yz, n_yz))

    loads = [
        pltpu.make_async_copy(src, dst, load_sem.at[i])
        for i, (src, dst) in enumerate(
            ((shift_hbm, shift), (kern_hbm, kern), (dens_hbm, dens), (ops_hbm, ops))
        )
    ]
    for load in loads:
        load.start()

    halo = [(da, db) for da in (-1, 0, 1) for db in (-1, 0, 1) if (da, db) != (0, 0)]
    partners = [(da, db % n_yz) for da, db in halo]
    partners += [(0, d) for d in range(1, n_yz) if (0, d) not in partners]
    partners += [(2, 0), (-2, 0)]
    barrier = pltpu.get_barrier_semaphore()
    for dg, dy in partners:
        pl.semaphore_signal(barrier, inc=1, device_id=at(dg, dy), device_id_type=MESH)

    pair = loct[...] * column + lpar[...]
    lanes = jnp.concatenate([pair] * leaf_side, axis=1)
    mine = iota(lanes.shape, 1) // leaf_side == iota(lanes.shape, 0)
    key_row = jnp.sum(jnp.where(mine, lanes, 0), axis=0, keepdims=True)
    child_hot = jnp.where(iota((octants * column, leaves), 0) == key_row, 1.0, 0.0).astype(BF16)
    children = dot(child_hot, mom[...]).astype(BF16)
    loads[0].wait()
    partial = jnp.zeros((column, coeffs), F32)
    for o in range(octants):
        partial += dot(children[o * column : (o + 1) * column], shift[o])
    part[yz] = partial
    win[4 * leaves : 5 * leaves, :] = mom[...]
    col_list[yz] = plist[...]
    col_op[yz] = pop[...]

    pl.semaphore_wait(barrier, len(partners))
    part_copies, list_copies, halo_copies, par_copies = [], [], [], []
    for d in range(1, n_yz):
        copy = pltpu.make_async_remote_copy(
            part.at[yz], part.at[yz], part_send.at[d - 1], part_recv.at[d - 1],
            device_id=at(0, d), device_id_type=MESH,
        )
        copy.start()
        part_copies.append(copy)
    for i, (da, db) in enumerate(halo):
        slot = (da + 1) * 3 + db + 1
        copy = pltpu.make_async_remote_copy(
            mom, win.at[pl.ds(slot * leaves, leaves)], halo_send.at[i], halo_recv.at[i],
            device_id=at(-da, -db), device_id_type=MESH,
        )
        copy.start()
        halo_copies.append(copy)
    for d in range(1, n_yz):
        for i, (src, dst) in enumerate(((plist, col_list), (pop, col_op))):
            copy = pltpu.make_async_remote_copy(
                src, dst.at[yz], list_send.at[i, d - 1], list_recv.at[i, d - 1],
                device_id=at(0, d), device_id_type=MESH,
            )
            copy.start()
            list_copies.append(copy)

    loads[1].wait()
    loads[2].wait()
    table[kinds * tiles] = jnp.zeros((shell, shell), F32)

    def products(j, carry):
        two = jnp.concatenate([dens[2 * j], dens[2 * j + 1]], axis=1)
        both = dot(kern[...].reshape(kinds * shell, shell), two)
        for k in range(kinds):
            rows = both[k * shell : (k + 1) * shell]
            table[k * tiles + 2 * j] = rows[:, :shell]
            table[k * tiles + 2 * j + 1] = rows[:, shell:]
        return carry

    lax.fori_loop(0, tiles // 2, products, 0)

    for copy in part_copies:
        copy.wait()
    moments = part[0]
    for d in range(1, n_yz):
        moments = moments + part[d]
    pwin[2 * column : 3 * column, :] = moments.astype(BF16)
    for i, d in enumerate((-2, -1, 1, 2)):
        copy = pltpu.make_async_remote_copy(
            pwin.at[pl.ds(2 * column, column)], pwin.at[pl.ds((d + 2) * column, column)],
            par_send.at[i], par_recv.at[i], device_id=at(-d, 0), device_id_type=MESH,
        )
        copy.start()
        par_copies.append(copy)

    def gather(t, carry):
        total = jnp.zeros((shell, shell), F32)
        for s in range(nsrc.shape[1]):
            place = jnp.where(s < ncount[t], nkind[t, s] * tiles + nsrc[t, s], kinds * tiles)
            total += table[place]
        near[t] = total
        return carry

    lax.fori_loop(0, tiles, gather, 0)

    repeat = jnp.where(iota((harm, coeffs), 0) == iota((harm, coeffs), 1) // harm, 1.0, 0.0)
    erep[...] = jnp.dot(erows[...], repeat, precision=lax.Precision.HIGHEST, preferred_element_type=F32)
    chigh, clow = split(jnp.concatenate([ecols[...]] * harm, axis=0))
    cboth[:, :shell] = chigh
    cboth[:, shell:] = clow

    def column_of(value):
        wide_value = jnp.broadcast_to(value[:, None, :], (leaf_side, leaf_side, leaf_side))
        diagonal = iota(wide_value.shape, 1) == iota(wide_value.shape, 2)
        return jnp.sum(jnp.where(diagonal, wide_value, 0), axis=2, keepdims=True).reshape(leaves, 1)

    parent_col = column_of(lpar[...])
    octant_col = column_of(loct[...])

    for copy in halo_copies:
        copy.wait()
    loads[3].wait()
    codes = llist[...]
    index = iota(codes.shape, 0)
    first = index // leaf_side + codes // span
    second = index % leaf_side + codes % span
    places = ((first // leaf_side) * 3 + second // leaf_side) * leaves
    places = places + (first % leaf_side) * leaf_side + second % leaf_side
    far[...] = listed_sum(win, places, lop[...], ops, hot, picked, wide, lhs)

    for copy in list_copies:
        copy.wait()
    for copy in par_copies:
        copy.wait()
    column_codes = col_list[...].reshape(column, plist.shape[1])
    column_ops = col_op[...].reshape(column, plist.shape[1])
    locals_ = listed_sum(pwin, column_codes, column_ops, ops, hot2, picked2, wide2, lhs2).astype(BF16)

    parent_hot = jnp.where(parent_col == iota((leaves, column), 1), 1.0, 0.0).astype(BF16)
    parent_rows = dot(parent_hot, locals_)
    lowered = far[...]
    for o in range(octants):
        chosen = jnp.where(octant_col == o, parent_rows, 0.0).astype(BF16)
        lowered += lax.dot_general(
            chosen, shift[o], (((1,), (1,)), ((), ())), preferred_element_type=F32
        )
    local[...] = lowered

    group = 4
    for start in range(0, tiles, group):
        boxes = local[start * box_tile : (start + group) * box_tile, :]
        spread = jnp.broadcast_to(boxes[:, None, :], (group * box_tile, shell // box_tile, coeffs))
        spread = spread.reshape(group, shell, coeffs) * erep[...][None]
        high, low = split(spread.reshape(group * shell, coeffs))
        main = dot(high, cboth[...])
        rest = dot(low, cboth[:, :shell])
        tile = (main[:, :shell] + main[:, shell:] + rest).reshape(group, shell, shell)
        out[start : start + group] = (tile + near[start : start + group]).astype(BF16)


def body(
    leaf_moments,
    leaf_list,
    leaf_op,
    leaf_parent,
    leaf_octant,
    parent_list,
    parent_op,
    operators,
    shift_up,
    density,
    nearby_coulomb_kernel,
    near_src,
    near_kind,
    near_count,
    eval_rows,
    eval_cols,
):
    n_gx, n_yz = lax.axis_size("gx"), lax.axis_size("yz")
    leaf_side, _, coeffs = leaf_moments.shape
    leaves = leaf_side * leaf_side
    slots = leaf_list.shape[2]
    per_dev, pslots = parent_list.shape[1:]
    column = per_dev * n_yz
    ops_count = operators.shape[0]
    tiles, shell, _ = density.shape
    kinds = nearby_coulomb_kernel.shape[0]
    vmem = pl.BlockSpec(memory_space=pltpu.VMEM)
    smem = pl.BlockSpec(memory_space=pltpu.SMEM)
    hbm = pl.BlockSpec(memory_space=pl.ANY)
    dma = pltpu.SemaphoreType.DMA
    return pl.pallas_call(
        functools.partial(kernel, n_gx, n_yz, leaf_side),
        out_shape=jax.ShapeDtypeStruct(density.shape, BF16),
        in_specs=[vmem] * 9 + [smem] * 3 + [hbm] * 4,
        out_specs=vmem,
        scratch_shapes=[
            pltpu.VMEM(operators.shape, BF16),
            pltpu.VMEM(shift_up.shape, BF16),
            pltpu.VMEM(density.shape, BF16),
            pltpu.VMEM(nearby_coulomb_kernel.shape, BF16),
            pltpu.VMEM((9 * leaves, coeffs), BF16),
            pltpu.VMEM((n_yz, per_dev, pslots), jnp.int32),
            pltpu.VMEM((n_yz, per_dev, pslots), jnp.int32),
            pltpu.VMEM((n_yz, column, coeffs), F32),
            pltpu.VMEM((5 * column, coeffs), BF16),
            pltpu.VMEM((kinds * tiles + 1, shell, shell), F32),
            pltpu.VMEM((tiles, shell, shell), F32),
            pltpu.VMEM((leaves, coeffs), F32),
            pltpu.VMEM((leaves, coeffs), F32),
            pltpu.VMEM((slots * leaves, 9 * leaves), BF16),
            pltpu.VMEM((slots * leaves, coeffs), F32),
            pltpu.VMEM((slots * leaves, 128), jnp.int32),
            pltpu.VMEM((2 * leaves, ops_count * coeffs), BF16),
            pltpu.VMEM((pslots * column, 5 * column), BF16),
            pltpu.VMEM((pslots * column, coeffs), F32),
            pltpu.VMEM((pslots * column, 128), jnp.int32),
            pltpu.VMEM((2 * column, ops_count * coeffs), BF16),
            pltpu.VMEM((shell, coeffs), F32),
            pltpu.VMEM((coeffs, 2 * shell), BF16),
            dma((4,)),
            dma((8,)),
            dma((8,)),
            dma((2, n_yz - 1)),
            dma((2, n_yz - 1)),
            dma((n_yz - 1,)),
            dma((n_yz - 1,)),
            dma((4,)),
            dma((4,)),
        ],
        compiler_params=pltpu.CompilerParams(
            collective_id=0, has_side_effects=True, vmem_limit_bytes=50 * 2**20
        ),
        name="fmm",
    )(
        leaf_moments.reshape(leaves, coeffs),
        leaf_list.reshape(leaves, slots),
        leaf_op.reshape(leaves, slots),
        leaf_parent,
        leaf_octant,
        parent_list[0],
        parent_op[0],
        eval_rows,
        eval_cols,
        near_src,
        near_kind,
        near_count,
        operators,
        shift_up,
        density,
        nearby_coulomb_kernel,
    )


def solution(mesh):
    in_specs = (
        P("gx", "yz", None),
        P("gx", "yz", None),
        P("gx", "yz", None),
        P("gx", "yz"),
        P("gx", "yz"),
        P("gx", "yz", None),
        P("gx", "yz", None),
        P(),
        P(),
        P(("gx", "yz"), None, None),
        P(),
        P(("gx", "yz"), None),
        P(("gx", "yz"), None),
        P(("gx", "yz")),
        P(),
        P(),
    )
    out_specs = P(("gx", "yz"), None, None)
    return jax.shard_map(body, mesh=mesh, in_specs=in_specs, out_specs=out_specs, check_vma=False)
```

```python
import functools

import jax
import jax.numpy as jnp
from jax import lax
from jax.experimental import pallas as pl
from jax.experimental.pallas import tpu as pltpu
from jax.sharding import PartitionSpec as P

MESH = pl.DeviceIdType.MESH
INPUTS = 16
F32 = jnp.float32
BF16 = jnp.bfloat16


def iota(shape, dim):
    return lax.broadcasted_iota(jnp.int32, shape, dim)


def dot(a, b):
    return jnp.dot(a, b, preferred_element_type=F32)


def split(value):
    high = value.astype(BF16)
    return high, (value - high.astype(F32)).astype(BF16)


def listed_sum(window_ref, codes, op_index, ops_ref, hot_ref, picked_ref, wide_ref, lhs_ref):
    rows, slots = codes.shape
    depth, coeffs = window_ref.shape
    ops_count = ops_ref.shape[0]
    places = iota((rows, depth), 1)
    for s in range(slots):
        hot_ref[s * rows : (s + 1) * rows, :] = jnp.where(
            codes[:, s : s + 1] == places, 1.0, 0.0
        ).astype(BF16)
    picked_ref[...] = dot(hot_ref[...], window_ref[...])
    for s in range(slots):
        wide_ref[s * rows : (s + 1) * rows, :] = jnp.broadcast_to(op_index[:, s : s + 1], (rows, 128))

    def collect(chunk, carry):
        base = pl.multiple_of(chunk * 16, 16)
        for half in range(coeffs // 128):
            lanes = slice(half * 128, (half + 1) * 128)
            for o in range(ops_count):
                total = jnp.zeros((16, 128), F32)
                for s in range(slots):
                    here = pl.ds(s * rows + base, 16)
                    total += jnp.where(wide_ref[here, :] == o, picked_ref[here, lanes], 0.0)
                high, low = split(total)
                at = o * coeffs + half * 128
                lhs_ref[pl.ds(base, 16), at : at + 128] = high
                lhs_ref[pl.ds(rows + base, 16), at : at + 128] = low
        return carry

    lax.fori_loop(0, rows // 16, collect, 0)
    both = dot(lhs_ref[...], ops_ref[...].reshape(ops_count * coeffs, coeffs))
    return both[:rows] + both[rows:]


def kernel(n_gx, n_yz, leaf_side, *refs):
    sources, out = refs[:INPUTS], refs[INPUTS]
    held = refs[INPUTS + 1 : 2 * INPUTS + 1]
    (mom, llist, lop, lpar, loct, plist, pop, ops, shift, dens, kern, nsrc, nkind, ncount,
     erows, ecols) = held
    (
    win, col_list, col_op, part, pwin,
    table, near, far, local,
    hot, picked, wide, lhs, hot2, picked2, wide2, lhs2,
    erep, cboth,
    load_sem, halo_send, halo_recv, list_send, list_recv, part_send, part_recv, par_send, par_recv,
    ) = refs[2 * INPUTS + 1 :]
    gx, yz = lax.axis_index("gx"), lax.axis_index("yz")
    leaves, coeffs = mom.shape
    kinds, shell = kern.shape[0], kern.shape[1]
    tiles = dens.shape[0]
    octants = shift.shape[0]
    column = part.shape[1]
    per_dev = plist.shape[0]
    harm = erows.shape[0]
    box_tile = leaves // tiles
    span = 2 * leaf_side + 1

    def at(dg, dy):
        return (lax.rem(gx + dg + 2 * n_gx, n_gx), lax.rem(yz + dy + n_yz, n_yz))

    loads = [
        pltpu.make_async_copy(src, dst, load_sem.at[i])
        for i, (src, dst) in enumerate(zip(sources, held))
    ]
    for i in (3, 4, 0, 8, 5, 6, 10, 9, 7, 11, 12, 13, 14, 15, 1, 2):
        loads[i].start()

    halo = [(da, db) for da in (-1, 0, 1) for db in (-1, 0, 1) if (da, db) != (0, 0)]
    partners = [(da, db % n_yz) for da, db in halo]
    partners += [(0, d) for d in range(1, n_yz) if (0, d) not in partners]
    partners += [(2, 0), (-2, 0)]
    barrier = pltpu.get_barrier_semaphore()
    for dg, dy in partners:
        pl.semaphore_signal(barrier, inc=1, device_id=at(dg, dy), device_id_type=MESH)

    for i in (3, 4, 0):
        loads[i].wait()
    pair = loct[...] * column + lpar[...]
    lanes = jnp.concatenate([pair] * leaf_side, axis=1)
    mine = iota(lanes.shape, 1) // leaf_side == iota(lanes.shape, 0)
    key_row = jnp.sum(jnp.where(mine, lanes, 0), axis=0, keepdims=True)
    child_hot = jnp.where(iota((octants * column, leaves), 0) == key_row, 1.0, 0.0).astype(BF16)
    children = dot(child_hot, mom[...]).astype(BF16)
    loads[8].wait()
    partial = jnp.zeros((column, coeffs), F32)
    for o in range(octants):
        partial += dot(children[o * column : (o + 1) * column], shift[o])
    part[yz] = partial
    loads[5].wait()
    loads[6].wait()
    win[4 * leaves : 5 * leaves, :] = mom[...]
    col_list[yz] = plist[...]
    col_op[yz] = pop[...]

    pl.semaphore_wait(barrier, len(partners))
    part_copies, list_copies, halo_copies, par_copies = [], [], [], []
    for d in range(1, n_yz):
        copy = pltpu.make_async_remote_copy(
            part.at[yz], part.at[yz], part_send.at[d - 1], part_recv.at[d - 1],
            device_id=at(0, d), device_id_type=MESH,
        )
        copy.start()
        part_copies.append(copy)
    for i, (da, db) in enumerate(halo):
        slot = (da + 1) * 3 + db + 1
        copy = pltpu.make_async_remote_copy(
            mom, win.at[pl.ds(slot * leaves, leaves)], halo_send.at[i], halo_recv.at[i],
            device_id=at(-da, -db), device_id_type=MESH,
        )
        copy.start()
        halo_copies.append(copy)
    for d in range(1, n_yz):
        for i, (src, dst) in enumerate(((plist, col_list), (pop, col_op))):
            copy = pltpu.make_async_remote_copy(
                src, dst.at[yz], list_send.at[i, d - 1], list_recv.at[i, d - 1],
                device_id=at(0, d), device_id_type=MESH,
            )
            copy.start()
            list_copies.append(copy)

    loads[10].wait()
    loads[9].wait()
    table[kinds * tiles] = jnp.zeros((shell, shell), F32)

    def products(j, carry):
        two = jnp.concatenate([dens[2 * j], dens[2 * j + 1]], axis=1)
        both = dot(kern[...].reshape(kinds * shell, shell), two)
        for k in range(kinds):
            rows = both[k * shell : (k + 1) * shell]
            table[k * tiles + 2 * j] = rows[:, :shell]
            table[k * tiles + 2 * j + 1] = rows[:, shell:]
        return carry

    lax.fori_loop(0, tiles // 2, products, 0)

    for copy in part_copies:
        copy.wait()
    moments = part[0]
    for d in range(1, n_yz):
        moments = moments + part[d]
    pwin[2 * column : 3 * column, :] = moments.astype(BF16)
    for i, d in enumerate((-2, -1, 1, 2)):
        copy = pltpu.make_async_remote_copy(
            pwin.at[pl.ds(2 * column, column)], pwin.at[pl.ds((d + 2) * column, column)],
            par_send.at[i], par_recv.at[i], device_id=at(-d, 0), device_id_type=MESH,
        )
        copy.start()
        par_copies.append(copy)

    for i in (11, 12, 13, 14, 15):
        loads[i].wait()

    def gather(t, carry):
        total = jnp.zeros((shell, shell), F32)
        for s in range(nsrc.shape[1]):
            place = jnp.where(s < ncount[t], nkind[t, s] * tiles + nsrc[t, s], kinds * tiles)
            total += table[place]
        near[t] = total
        return carry

    lax.fori_loop(0, tiles, gather, 0)

    repeat = jnp.where(iota((harm, coeffs), 0) == iota((harm, coeffs), 1) // harm, 1.0, 0.0)
    erep[...] = lax.dot_general(
        erows[...], repeat, (((0,), (0,)), ((), ())),
        precision=lax.Precision.HIGHEST, preferred_element_type=F32,
    )
    chigh, clow = split(jnp.concatenate([ecols[...]] * harm, axis=0))
    cboth[:, :shell] = chigh
    cboth[:, shell:] = clow

    def column_of(value):
        wide_value = jnp.broadcast_to(value[:, None, :], (leaf_side, leaf_side, leaf_side))
        diagonal = iota(wide_value.shape, 1) == iota(wide_value.shape, 2)
        return jnp.sum(jnp.where(diagonal, wide_value, 0), axis=2, keepdims=True).reshape(leaves, 1)

    parent_col = column_of(lpar[...])
    octant_col = column_of(loct[...])

    for copy in halo_copies:
        copy.wait()
    for i in (7, 1, 2):
        loads[i].wait()
    codes = llist[...]
    index = iota(codes.shape, 0)
    first = index // leaf_side + codes // span
    second = index % leaf_side + codes % span
    places = ((first // leaf_side) * 3 + second // leaf_side) * leaves
    places = places + (first % leaf_side) * leaf_side + second % leaf_side
    far[...] = listed_sum(win, places, lop[...], ops, hot, picked, wide, lhs)

    for copy in list_copies:
        copy.wait()
    for copy in par_copies:
        copy.wait()
    column_codes = col_list[...].reshape(column, plist.shape[1])
    column_ops = col_op[...].reshape(column, plist.shape[1])
    locals_ = listed_sum(pwin, column_codes, column_ops, ops, hot2, picked2, wide2, lhs2).astype(BF16)

    parent_hot = jnp.where(parent_col == iota((leaves, column), 1), 1.0, 0.0).astype(BF16)
    parent_rows = dot(parent_hot, locals_)
    lowered = far[...]
    for o in range(octants):
        chosen = jnp.where(octant_col == o, parent_rows, 0.0).astype(BF16)
        lowered += lax.dot_general(
            chosen, shift[o], (((1,), (1,)), ((), ())), preferred_element_type=F32
        )
    local[...] = lowered

    group = 4
    for start in range(0, tiles, group):
        boxes = local[start * box_tile : (start + group) * box_tile, :]
        spread = jnp.broadcast_to(boxes[:, None, :], (group * box_tile, shell // box_tile, coeffs))
        spread = spread.reshape(group, shell, coeffs) * erep[...][None]
        high, low = split(spread.reshape(group * shell, coeffs))
        main = dot(high, cboth[...])
        rest = dot(low, cboth[:, :shell])
        tile = (main[:, :shell] + main[:, shell:] + rest).reshape(group, shell, shell)
        out[start : start + group] = (tile + near[start : start + group]).astype(BF16)


def body(
    leaf_moments,
    leaf_list,
    leaf_op,
    leaf_parent,
    leaf_octant,
    parent_list,
    parent_op,
    operators,
    shift_up,
    density,
    nearby_coulomb_kernel,
    near_src,
    near_kind,
    near_count,
    eval_rows,
    eval_cols,
):
    n_gx, n_yz = lax.axis_size("gx"), lax.axis_size("yz")
    leaf_side, _, coeffs = leaf_moments.shape
    leaves = leaf_side * leaf_side
    slots = leaf_list.shape[2]
    per_dev, pslots = parent_list.shape[1:]
    column = per_dev * n_yz
    ops_count = operators.shape[0]
    tiles, shell, _ = density.shape
    kinds = nearby_coulomb_kernel.shape[0]
    inputs = (
        leaf_moments.reshape(leaves, coeffs),
        leaf_list.reshape(leaves, slots),
        leaf_op.reshape(leaves, slots),
        leaf_parent,
        leaf_octant,
        parent_list[0],
        parent_op[0],
        operators,
        shift_up,
        density,
        nearby_coulomb_kernel,
        near_src,
        near_kind,
        near_count,
        eval_rows.T,
        eval_cols,
    )
    vmem = pl.BlockSpec(memory_space=pltpu.VMEM)
    hbm = pl.BlockSpec(memory_space=pltpu.HBM)
    dma = pltpu.SemaphoreType.DMA
    return pl.pallas_call(
        functools.partial(kernel, n_gx, n_yz, leaf_side),
        out_shape=jax.ShapeDtypeStruct(density.shape, BF16),
        in_specs=[hbm] * INPUTS,
        out_specs=vmem,
        scratch_shapes=[
            *(
                (pltpu.SMEM if i in (11, 12, 13) else pltpu.VMEM)(value.shape, value.dtype)
                for i, value in enumerate(inputs)
            ),
            pltpu.VMEM((9 * leaves, coeffs), BF16),
            pltpu.VMEM((n_yz, per_dev, pslots), jnp.int32),
            pltpu.VMEM((n_yz, per_dev, pslots), jnp.int32),
            pltpu.VMEM((n_yz, column, coeffs), F32),
            pltpu.VMEM((5 * column, coeffs), BF16),
            pltpu.VMEM((kinds * tiles + 1, shell, shell), F32),
            pltpu.VMEM((tiles, shell, shell), F32),
            pltpu.VMEM((leaves, coeffs), F32),
            pltpu.VMEM((leaves, coeffs), F32),
            pltpu.VMEM((slots * leaves, 9 * leaves), BF16),
            pltpu.VMEM((slots * leaves, coeffs), F32),
            pltpu.VMEM((slots * leaves, 128), jnp.int32),
            pltpu.VMEM((2 * leaves, ops_count * coeffs), BF16),
            pltpu.VMEM((pslots * column, 5 * column), BF16),
            pltpu.VMEM((pslots * column, coeffs), F32),
            pltpu.VMEM((pslots * column, 128), jnp.int32),
            pltpu.VMEM((2 * column, ops_count * coeffs), BF16),
            pltpu.VMEM((shell, coeffs), F32),
            pltpu.VMEM((coeffs, 2 * shell), BF16),
            dma((INPUTS,)),
            dma((8,)),
            dma((8,)),
            dma((2, n_yz - 1)),
            dma((2, n_yz - 1)),
            dma((n_yz - 1,)),
            dma((n_yz - 1,)),
            dma((4,)),
            dma((4,)),
        ],
        compiler_params=pltpu.CompilerParams(
            collective_id=0, has_side_effects=True, vmem_limit_bytes=60 * 2**20
        ),
        name="fmm",
    )(*inputs)


def solution(mesh):
    in_specs = (
        P("gx", "yz", None),
        P("gx", "yz", None),
        P("gx", "yz", None),
        P("gx", "yz"),
        P("gx", "yz"),
        P("gx", "yz", None),
        P("gx", "yz", None),
        P(),
        P(),
        P(("gx", "yz"), None, None),
        P(),
        P(("gx", "yz"), None),
        P(("gx", "yz"), None),
        P(("gx", "yz")),
        P(),
        P(),
    )
    out_specs = P(("gx", "yz"), None, None)
    return jax.shard_map(body, mesh=mesh, in_specs=in_specs, out_specs=out_specs, check_vma=False)
```

```python
import functools

import jax
import jax.numpy as jnp
from jax import lax
from jax.experimental import pallas as pl
from jax.experimental.pallas import tpu as pltpu
from jax.sharding import PartitionSpec as P

MESH = pl.DeviceIdType.MESH
INPUTS = 16
GROUP = 16
F32 = jnp.float32
BF16 = jnp.bfloat16


def iota(shape, dim):
    return lax.broadcasted_iota(jnp.int32, shape, dim)


def dot(a, b):
    return jnp.dot(a, b, preferred_element_type=F32)


def split(value):
    high = value.astype(BF16)
    return high, (value - high.astype(F32)).astype(BF16)


def place_hot(codes, depth, hot_ref):
    rows, slots = codes.shape
    places = iota((GROUP, depth), 1)
    for start in range(0, rows, GROUP):
        for s in range(slots):
            base = start * slots + s * GROUP
            hot_ref[base : base + GROUP, :] = jnp.where(
                codes[start : start + GROUP, s : s + 1] == places, 1.0, 0.0
            ).astype(BF16)


def operator_hot(op_index, ops_count, key_ref):
    rows, slots = op_index.shape
    width = slots * GROUP
    repeat = jnp.where(iota((slots, width), 0) == iota((slots, width), 1) // GROUP, 1.0, 0.0)
    spread = dot(op_index.astype(F32).astype(BF16), repeat.astype(BF16))
    shape = (GROUP, width)
    mine = iota(shape, 0) == iota(shape, 1) % GROUP
    own = iota((1, width), 1) % GROUP
    for group in range(rows // GROUP):
        one = spread[group * GROUP : (group + 1) * GROUP]
        key = jnp.sum(jnp.where(mine, one, 0.0), axis=0, keepdims=True).astype(jnp.int32)
        key = key * GROUP + own
        key_ref[group] = jnp.where(iota((ops_count * GROUP, width), 0) == key, 1.0, 0.0).astype(BF16)


def listed_sum(window_ref, ops_ref, hot_ref, key_ref, lhs_ref):
    groups, _, width = key_ref.shape
    ops_count, coeffs, _ = ops_ref.shape
    rows = groups * GROUP
    for group in range(groups):
        picked = dot(hot_ref[group * width : (group + 1) * width, :], window_ref[...]).astype(BF16)
        high, low = split(dot(key_ref[group], picked))
        for o in range(ops_count):
            here = slice(o * GROUP, (o + 1) * GROUP)
            lanes = slice(o * coeffs, (o + 1) * coeffs)
            lhs_ref[group * GROUP : (group + 1) * GROUP, lanes] = high[here]
            lhs_ref[rows + group * GROUP : rows + (group + 1) * GROUP, lanes] = low[here]
    both = dot(lhs_ref[...], ops_ref[...].reshape(ops_count * coeffs, coeffs))
    return both[:rows] + both[rows:]


def kernel(n_gx, n_yz, leaf_side, *refs):
    sources, out = refs[:INPUTS], refs[INPUTS]
    held = refs[INPUTS + 1 : 2 * INPUTS + 1]
    (mom, llist, lop, lpar, loct, plist, pop, ops, shift, dens, kern, nsrc, nkind, ncount,
     erows, ecols) = held
    (
    win, col_list, col_op, part, pwin,
    table, near, far,
    hot, key, lhs, hot2, key2, lhs2,
    esix, cboth, leaf_rows,
    load_sem, halo_send, halo_recv, list_send, list_recv, part_send, part_recv, par_send, par_recv,
    ) = refs[2 * INPUTS + 1 :]
    gx, yz = lax.axis_index("gx"), lax.axis_index("yz")
    leaves, coeffs = mom.shape
    kinds, shell = kern.shape[0], kern.shape[1]
    tiles = dens.shape[0]
    octants = shift.shape[0]
    column = part.shape[1]
    per_dev = plist.shape[0]
    harm = erows.shape[0]
    box_tile = leaves // tiles
    span = 2 * leaf_side + 1

    def at(dg, dy):
        return (lax.rem(gx + dg + 2 * n_gx, n_gx), lax.rem(yz + dy + n_yz, n_yz))

    loads = [
        pltpu.make_async_copy(src, dst, load_sem.at[i])
        for i, (src, dst) in enumerate(zip(sources, held))
    ]
    for i in (3, 4, 0, 8, 5, 6, 11, 12, 13, 14, 15, 1, 2):
        loads[i].start()

    halo = [(da, db) for da in (-1, 0, 1) for db in (-1, 0, 1) if (da, db) != (0, 0)]
    partners = [(da, db % n_yz) for da, db in halo]
    partners += [(0, d) for d in range(1, n_yz) if (0, d) not in partners]
    partners += [(2, 0), (-2, 0)]
    barrier = pltpu.get_barrier_semaphore()
    for dg, dy in partners:
        pl.semaphore_signal(barrier, inc=1, device_id=at(dg, dy), device_id_type=MESH)

    for i in (3, 4, 0):
        loads[i].wait()
    pair = loct[...] * column + lpar[...]
    lanes = jnp.concatenate([pair] * leaf_side, axis=1)
    mine = iota(lanes.shape, 1) // leaf_side == iota(lanes.shape, 0)
    key_row = jnp.sum(jnp.where(mine, lanes, 0), axis=0, keepdims=True)
    child_hot = jnp.where(iota((octants * column, leaves), 0) == key_row, 1.0, 0.0).astype(BF16)
    children = dot(child_hot, mom[...]).astype(BF16)
    loads[8].wait()
    for i in (10, 9, 7):
        loads[i].start()
    partial = jnp.zeros((column, coeffs), F32)
    for o in range(octants):
        partial += dot(children[o * column : (o + 1) * column], shift[o])
    part[yz] = partial
    loads[5].wait()
    loads[6].wait()
    win[4 * leaves : 5 * leaves, :] = mom[...]
    col_list[yz] = plist[...]
    col_op[yz] = pop[...]

    pl.semaphore_wait(barrier, len(partners))
    part_copies, list_copies, halo_copies, par_copies = [], [], [], []
    for d in range(1, n_yz):
        copy = pltpu.make_async_remote_copy(
            part.at[yz], part.at[yz], part_send.at[d - 1], part_recv.at[d - 1],
            device_id=at(0, d), device_id_type=MESH,
        )
        copy.start()
        part_copies.append(copy)
    for i, (da, db) in enumerate(halo):
        slot = (da + 1) * 3 + db + 1
        copy = pltpu.make_async_remote_copy(
            mom, win.at[pl.ds(slot * leaves, leaves)], halo_send.at[i], halo_recv.at[i],
            device_id=at(-da, -db), device_id_type=MESH,
        )
        copy.start()
        halo_copies.append(copy)
    for d in range(1, n_yz):
        for i, (src, dst) in enumerate(((plist, col_list), (pop, col_op))):
            copy = pltpu.make_async_remote_copy(
                src, dst.at[yz], list_send.at[i, d - 1], list_recv.at[i, d - 1],
                device_id=at(0, d), device_id_type=MESH,
            )
            copy.start()
            list_copies.append(copy)

    loads[10].wait()
    loads[9].wait()
    table[kinds * tiles] = jnp.zeros((shell, shell), F32)

    def products(j, carry):
        two = jnp.concatenate([dens[2 * j], dens[2 * j + 1]], axis=1)
        both = dot(kern[...].reshape(kinds * shell, shell), two)
        for k in range(kinds):
            rows = both[k * shell : (k + 1) * shell]
            table[k * tiles + 2 * j] = rows[:, :shell]
            table[k * tiles + 2 * j + 1] = rows[:, shell:]
        return carry

    lax.fori_loop(0, tiles // 2, products, 0)

    for i in (11, 12, 13, 14, 15, 1, 2):
        loads[i].wait()

    repeat = jnp.where(iota((harm, box_tile * harm), 0) == iota((harm, box_tile * harm), 1) % harm, 1.0, 0.0)
    rows_wide = lax.dot_general(
        erows[...], repeat, (((0,), (0,)), ((), ())),
        precision=lax.Precision.HIGHEST, preferred_element_type=F32,
    )
    block = iota(rows_wide.shape, 0) // (shell // box_tile) == iota(rows_wide.shape, 1) // harm
    rhigh, rlow = split(jnp.where(block, rows_wide, 0.0))
    esix[...] = jnp.concatenate([rhigh, rlow, rhigh], axis=1)
    chigh, clow = split(jnp.concatenate([ecols[...]] * harm, axis=0))
    cboth[:, :shell] = chigh
    cboth[:, shell:] = clow

    def column_of(value):
        wide_value = jnp.broadcast_to(value[:, None, :], (leaf_side, leaf_side, leaf_side))
        diagonal = iota(wide_value.shape, 1) == iota(wide_value.shape, 2)
        return jnp.sum(jnp.where(diagonal, wide_value, 0), axis=2, keepdims=True).reshape(leaves, 1)

    parent_col = column_of(lpar[...])
    octant_col = column_of(loct[...])
    parent_hot = jnp.where(parent_col == iota((leaves, column), 1), 1.0, 0.0).astype(BF16)

    codes = llist[...]
    index = iota(codes.shape, 0)
    first = index // leaf_side + codes // span
    second = index % leaf_side + codes % span
    places = ((first // leaf_side) * 3 + second // leaf_side) * leaves
    places = places + (first % leaf_side) * leaf_side + second % leaf_side
    place_hot(places, 9 * leaves, hot)
    operator_hot(lop[...], ops.shape[0], key)

    for copy in part_copies:
        copy.wait()
    moments = part[0]
    for d in range(1, n_yz):
        moments = moments + part[d]
    pwin[2 * column : 3 * column, :] = moments.astype(BF16)
    for i, d in enumerate((-2, -1, 1, 2)):
        copy = pltpu.make_async_remote_copy(
            pwin.at[pl.ds(2 * column, column)], pwin.at[pl.ds((d + 2) * column, column)],
            par_send.at[i], par_recv.at[i], device_id=at(-d, 0), device_id_type=MESH,
        )
        copy.start()
        par_copies.append(copy)

    def gather(t, carry):
        total = jnp.zeros((shell, shell), F32)
        for s in range(nsrc.shape[1]):
            place = jnp.where(s < ncount[t], nkind[t, s] * tiles + nsrc[t, s], kinds * tiles)
            total += table[place]
        near[t] = total
        return carry

    lax.fori_loop(0, tiles, gather, 0)

    for copy in halo_copies:
        copy.wait()
    loads[7].wait()
    far[...] = listed_sum(win, ops, hot, key, lhs)

    for copy in list_copies:
        copy.wait()
    place_hot(col_list[...].reshape(column, plist.shape[1]), 5 * column, hot2)
    operator_hot(col_op[...].reshape(column, plist.shape[1]), ops.shape[0], key2)
    for copy in par_copies:
        copy.wait()
    locals_ = listed_sum(pwin, ops, hot2, key2, lhs2).astype(BF16)

    parent_rows = dot(parent_hot, locals_)
    lowered = far[...]
    for o in range(octants):
        chosen = jnp.where(octant_col == o, parent_rows, 0.0).astype(BF16)
        lowered += lax.dot_general(
            chosen, shift[o], (((1,), (1,)), ((), ())), preferred_element_type=F32
        )
    own_lanes = iota((harm, coeffs), 1) // harm == iota((harm, coeffs), 0)
    for part_number, value in enumerate(split(lowered)):
        value = value.astype(F32)
        for n in range(leaves):
            row = jnp.broadcast_to(value[n : n + 1], (harm, coeffs))
            leaf_rows[part_number, n * harm : (n + 1) * harm, :] = jnp.where(
                own_lanes, row, 0.0
            ).astype(BF16)
    group = box_tile * harm
    step = 4
    for start in range(0, tiles, step):
        here = slice(start * group, (start + step) * group)
        main = dot(leaf_rows[0, here, :], cboth[...])
        value = main[:, :shell] + main[:, shell:] + dot(leaf_rows[1, here, :], cboth[:, :shell])
        high, low = split(value)
        for t in range(0, step, 2):
            pair_rhs = []
            for u in (t, t + 1):
                rows = slice(u * group, (u + 1) * group)
                pair_rhs.append(jnp.concatenate([high[rows], high[rows], low[rows]], axis=0))
            both = dot(esix[...], jnp.concatenate(pair_rhs, axis=1))
            out[start + t] = (both[:, :shell] + near[start + t]).astype(BF16)
            out[start + t + 1] = (both[:, shell:] + near[start + t + 1]).astype(BF16)


def body(
    leaf_moments,
    leaf_list,
    leaf_op,
    leaf_parent,
    leaf_octant,
    parent_list,
    parent_op,
    operators,
    shift_up,
    density,
    nearby_coulomb_kernel,
    near_src,
    near_kind,
    near_count,
    eval_rows,
    eval_cols,
):
    n_gx, n_yz = lax.axis_size("gx"), lax.axis_size("yz")
    leaf_side, _, coeffs = leaf_moments.shape
    leaves = leaf_side * leaf_side
    slots = leaf_list.shape[2]
    per_dev, pslots = parent_list.shape[1:]
    column = per_dev * n_yz
    ops_count = operators.shape[0]
    tiles, shell, _ = density.shape
    kinds = nearby_coulomb_kernel.shape[0]
    inputs = (
        leaf_moments.reshape(leaves, coeffs),
        leaf_list.reshape(leaves, slots),
        leaf_op.reshape(leaves, slots),
        leaf_parent,
        leaf_octant,
        parent_list[0],
        parent_op[0],
        operators,
        shift_up,
        density,
        nearby_coulomb_kernel,
        near_src,
        near_kind,
        near_count,
        eval_rows.T,
        eval_cols,
    )
    vmem = pl.BlockSpec(memory_space=pltpu.VMEM)
    hbm = pl.BlockSpec(memory_space=pltpu.HBM)
    dma = pltpu.SemaphoreType.DMA
    return pl.pallas_call(
        functools.partial(kernel, n_gx, n_yz, leaf_side),
        out_shape=jax.ShapeDtypeStruct(density.shape, BF16),
        in_specs=[hbm] * INPUTS,
        out_specs=vmem,
        scratch_shapes=[
            *(
                (pltpu.SMEM if i in (11, 12, 13) else pltpu.VMEM)(value.shape, value.dtype)
                for i, value in enumerate(inputs)
            ),
            pltpu.VMEM((9 * leaves, coeffs), BF16),
            pltpu.VMEM((n_yz, per_dev, pslots), jnp.int32),
            pltpu.VMEM((n_yz, per_dev, pslots), jnp.int32),
            pltpu.VMEM((n_yz, column, coeffs), F32),
            pltpu.VMEM((5 * column, coeffs), BF16),
            pltpu.VMEM((kinds * tiles + 1, shell, shell), F32),
            pltpu.VMEM((tiles, shell, shell), F32),
            pltpu.VMEM((leaves, coeffs), F32),
            pltpu.VMEM((slots * leaves, 9 * leaves), BF16),
            pltpu.VMEM((leaves // GROUP, ops_count * GROUP, slots * GROUP), BF16),
            pltpu.VMEM((2 * leaves, ops_count * coeffs), BF16),
            pltpu.VMEM((pslots * column, 5 * column), BF16),
            pltpu.VMEM((column // GROUP, ops_count * GROUP, pslots * GROUP), BF16),
            pltpu.VMEM((2 * column, ops_count * coeffs), BF16),
            pltpu.VMEM((shell, 3 * leaves // tiles * eval_rows.shape[1]), BF16),
            pltpu.VMEM((coeffs, 2 * shell), BF16),
            pltpu.VMEM((2, leaves * eval_rows.shape[1], coeffs), BF16),
            dma((INPUTS,)),
            dma((8,)),
            dma((8,)),
            dma((2, n_yz - 1)),
            dma((2, n_yz - 1)),
            dma((n_yz - 1,)),
            dma((n_yz - 1,)),
            dma((4,)),
            dma((4,)),
        ],
        compiler_params=pltpu.CompilerParams(
            collective_id=0, has_side_effects=True, vmem_limit_bytes=32 * 2**20
        ),
        name="fmm",
    )(*inputs)


def solution(mesh):
    in_specs = (
        P("gx", "yz", None),
        P("gx", "yz", None),
        P("gx", "yz", None),
        P("gx", "yz"),
        P("gx", "yz"),
        P("gx", "yz", None),
        P("gx", "yz", None),
        P(),
        P(),
        P(("gx", "yz"), None, None),
        P(),
        P(("gx", "yz"), None),
        P(("gx", "yz"), None),
        P(("gx", "yz")),
        P(),
        P(),
    )
    out_specs = P(("gx", "yz"), None, None)
    return jax.shard_map(body, mesh=mesh, in_specs=in_specs, out_specs=out_specs, check_vma=False)
```

```python
import functools

import jax
import jax.numpy as jnp
from jax import lax
from jax.experimental import pallas as pl
from jax.experimental.pallas import tpu as pltpu
from jax.sharding import PartitionSpec as P

MESH = pl.DeviceIdType.MESH
INPUTS = 16
GROUP = 16
F32 = jnp.float32
BF16 = jnp.bfloat16


def iota(shape, dim):
    return lax.broadcasted_iota(jnp.int32, shape, dim)


def dot(a, b):
    return jnp.dot(a, b, preferred_element_type=F32)


def split(value):
    high = value.astype(BF16)
    return high, (value - high.astype(F32)).astype(BF16)


def place_hot(codes, depth, hot_ref):
    rows, slots = codes.shape
    places = iota((GROUP, depth), 1)
    for start in range(0, rows, GROUP):
        for s in range(slots):
            base = start * slots + s * GROUP
            hot_ref[base : base + GROUP, :] = jnp.where(
                codes[start : start + GROUP, s : s + 1] == places, 1.0, 0.0
            ).astype(BF16)


def operator_hot(op_index, ops_count, key_ref):
    rows, slots = op_index.shape
    width = slots * GROUP
    repeat = jnp.where(iota((slots, width), 0) == iota((slots, width), 1) // GROUP, 1.0, 0.0)
    spread = dot(op_index.astype(F32).astype(BF16), repeat.astype(BF16))
    shape = (GROUP, width)
    mine = iota(shape, 0) == iota(shape, 1) % GROUP
    own = iota((1, width), 1) % GROUP
    for group in range(rows // GROUP):
        one = spread[group * GROUP : (group + 1) * GROUP]
        key = jnp.sum(jnp.where(mine, one, 0.0), axis=0, keepdims=True).astype(jnp.int32)
        key = key * GROUP + own
        key_ref[group] = jnp.where(iota((ops_count * GROUP, width), 0) == key, 1.0, 0.0).astype(BF16)


def listed_sum(window_ref, ops_ref, hot_ref, key_ref, picked_ref, lhs_ref):
    groups, _, width = key_ref.shape
    ops_count, coeffs, _ = ops_ref.shape
    rows = groups * GROUP
    picked_ref[...] = dot(hot_ref[...], window_ref[...]).astype(BF16)
    for group in range(groups):
        picked = picked_ref[group * width : (group + 1) * width, :]
        high, low = split(dot(key_ref[group], picked))
        for o in range(ops_count):
            here = slice(o * GROUP, (o + 1) * GROUP)
            lanes = slice(o * coeffs, (o + 1) * coeffs)
            lhs_ref[group * GROUP : (group + 1) * GROUP, lanes] = high[here]
            lhs_ref[rows + group * GROUP : rows + (group + 1) * GROUP, lanes] = low[here]
    both = dot(lhs_ref[...], ops_ref[...].reshape(ops_count * coeffs, coeffs))
    return both[:rows] + both[rows:]


def kernel(n_gx, n_yz, leaf_side, *refs):
    sources, out = refs[:INPUTS], refs[INPUTS]
    held = refs[INPUTS + 1 : 2 * INPUTS + 1]
    (mom, llist, lop, lpar, loct, plist, pop, ops, shift, dens, kern, nsrc, nkind, ncount,
     erows, ecols) = held
    (
    win, col_list, col_op, part, pwin,
    table, near, far,
    hot, key, picked, lhs, hot2, key2, picked2, lhs2,
    esix, cboth, leaf_rows, values,
    load_sem, halo_send, halo_recv, list_send, list_recv, part_send, part_recv, par_send, par_recv,
    ) = refs[2 * INPUTS + 1 :]
    gx, yz = lax.axis_index("gx"), lax.axis_index("yz")
    leaves, coeffs = mom.shape
    kinds, shell = kern.shape[0], kern.shape[1]
    tiles = dens.shape[0]
    octants = shift.shape[0]
    column = part.shape[1]
    per_dev = plist.shape[0]
    harm = erows.shape[0]
    box_tile = leaves // tiles
    span = 2 * leaf_side + 1

    def at(dg, dy):
        return (lax.rem(gx + dg + 2 * n_gx, n_gx), lax.rem(yz + dy + n_yz, n_yz))

    loads = [
        pltpu.make_async_copy(src, dst, load_sem.at[i])
        for i, (src, dst) in enumerate(zip(sources, held))
    ]
    for i in (3, 4, 0, 8, 5, 6, 11, 12, 13, 14, 15, 1, 2):
        loads[i].start()

    partners = [(0, d) for d in range(1, n_yz)] + [(d, 0) for d in (-2, -1, 1, 2)]
    barrier = pltpu.get_barrier_semaphore()
    for dg, dy in partners:
        pl.semaphore_signal(barrier, inc=1, device_id=at(dg, dy), device_id_type=MESH)

    for i in (3, 4, 0):
        loads[i].wait()
    pair = loct[...] * column + lpar[...]
    lanes = jnp.concatenate([pair] * leaf_side, axis=1)
    mine = iota(lanes.shape, 1) // leaf_side == iota(lanes.shape, 0)
    key_row = jnp.sum(jnp.where(mine, lanes, 0), axis=0, keepdims=True)
    child_hot = jnp.where(iota((octants * column, leaves), 0) == key_row, 1.0, 0.0).astype(BF16)
    children = dot(child_hot, mom[...]).astype(BF16)
    loads[8].wait()
    for i in (10, 9, 7):
        loads[i].start()
    partial = jnp.zeros((column, coeffs), F32)
    for o in range(octants):
        partial += dot(children[o * column : (o + 1) * column], shift[o])
    part[yz] = partial
    loads[5].wait()
    loads[6].wait()
    win[4 * leaves : 5 * leaves, :] = mom[...]
    col_list[yz] = plist[...]
    col_op[yz] = pop[...]

    pl.semaphore_wait(barrier, len(partners))
    part_copies, list_copies, halo_copies, par_copies = [], [], [], []
    for d in range(1, n_yz):
        copy = pltpu.make_async_remote_copy(
            part.at[yz], part.at[yz], part_send.at[d - 1], part_recv.at[d - 1],
            device_id=at(0, d), device_id_type=MESH,
        )
        copy.start()
        part_copies.append(copy)
    def window_at(da, db):
        return win.at[pl.ds(((da + 1) * 3 + db + 1) * leaves, leaves)]

    def halo_copy(i, src, dst, dg, dy):
        return pltpu.make_async_remote_copy(
            src, dst, halo_send.at[i], halo_recv.at[i],
            device_id=at(dg, dy), device_id_type=MESH,
        )

    side_copies = [halo_copy(i, mom, window_at(0, d), 0, -d) for i, d in enumerate((-1, 1))]
    halo_copies = [halo_copy(i + 2, mom, window_at(d, 0), -d, 0) for i, d in enumerate((-1, 1))]
    for copy in side_copies + halo_copies:
        copy.start()
    for d in range(1, n_yz):
        for i, (src, dst) in enumerate(((plist, col_list), (pop, col_op))):
            copy = pltpu.make_async_remote_copy(
                src, dst.at[yz], list_send.at[i, d - 1], list_recv.at[i, d - 1],
                device_id=at(0, d), device_id_type=MESH,
            )
            copy.start()
            list_copies.append(copy)

    loads[10].wait()
    loads[9].wait()
    table[kinds * tiles] = jnp.zeros((shell, shell), F32)

    def products(j, carry):
        two = jnp.concatenate([dens[2 * j], dens[2 * j + 1]], axis=1)
        both = dot(kern[...].reshape(kinds * shell, shell), two)
        for k in range(kinds):
            rows = both[k * shell : (k + 1) * shell]
            table[k * tiles + 2 * j] = rows[:, :shell]
            table[k * tiles + 2 * j + 1] = rows[:, shell:]
        return carry

    lax.fori_loop(0, tiles // 2, products, 0)

    for i in (11, 12, 13, 14, 15, 1, 2):
        loads[i].wait()

    repeat = jnp.where(iota((harm, box_tile * harm), 0) == iota((harm, box_tile * harm), 1) % harm, 1.0, 0.0)
    rows_wide = lax.dot_general(
        erows[...], repeat, (((0,), (0,)), ((), ())),
        precision=lax.Precision.HIGHEST, preferred_element_type=F32,
    )
    block = iota(rows_wide.shape, 0) // (shell // box_tile) == iota(rows_wide.shape, 1) // harm
    rhigh, rlow = split(jnp.where(block, rows_wide, 0.0))
    esix[...] = jnp.concatenate([rhigh, rlow, rhigh], axis=1)
    chigh, clow = split(jnp.concatenate([ecols[...]] * harm, axis=0))
    cboth[:, :shell] = chigh
    cboth[:, shell:] = clow

    def column_of(value):
        wide_value = jnp.broadcast_to(value[:, None, :], (leaf_side, leaf_side, leaf_side))
        diagonal = iota(wide_value.shape, 1) == iota(wide_value.shape, 2)
        return jnp.sum(jnp.where(diagonal, wide_value, 0), axis=2, keepdims=True).reshape(leaves, 1)

    parent_col = column_of(lpar[...])
    octant_col = column_of(loct[...])
    parent_hot = jnp.where(parent_col == iota((leaves, column), 1), 1.0, 0.0).astype(BF16)

    codes = llist[...]
    index = iota(codes.shape, 0)
    first = index // leaf_side + codes // span
    second = index % leaf_side + codes % span
    places = ((first // leaf_side) * 3 + second // leaf_side) * leaves
    places = places + (first % leaf_side) * leaf_side + second % leaf_side
    place_hot(places, 9 * leaves, hot)
    operator_hot(lop[...], ops.shape[0], key)

    for copy in part_copies:
        copy.wait()
    moments = part[0]
    for d in range(1, n_yz):
        moments = moments + part[d]
    pwin[2 * column : 3 * column, :] = moments.astype(BF16)
    for i, d in enumerate((-2, -1, 1, 2)):
        copy = pltpu.make_async_remote_copy(
            pwin.at[pl.ds(2 * column, column)], pwin.at[pl.ds((d + 2) * column, column)],
            par_send.at[i], par_recv.at[i], device_id=at(-d, 0), device_id_type=MESH,
        )
        copy.start()
        par_copies.append(copy)

    for i, db in enumerate((-1, 1)):
        side_copies[i].wait()
        for j, da in enumerate((-1, 1)):
            copy = halo_copy(4 + 2 * i + j, window_at(0, db), window_at(da, db), -da, 0)
            copy.start()
            halo_copies.append(copy)

    def gather(t, carry):
        total = jnp.zeros((shell, shell), F32)
        for s in range(nsrc.shape[1]):
            place = jnp.where(s < ncount[t], nkind[t, s] * tiles + nsrc[t, s], kinds * tiles)
            total += table[place]
        near[t] = total
        return carry

    lax.fori_loop(0, tiles, gather, 0)

    loads[7].wait()
    for copy in list_copies:
        copy.wait()
    place_hot(col_list[...].reshape(column, plist.shape[1]), 5 * column, hot2)
    operator_hot(col_op[...].reshape(column, plist.shape[1]), ops.shape[0], key2)
    for copy in par_copies:
        copy.wait()
    locals_ = listed_sum(pwin, ops, hot2, key2, picked2, lhs2).astype(BF16)

    parent_rows = dot(parent_hot, locals_)
    lowered = jnp.zeros((leaves, coeffs), F32)
    for o in range(octants):
        chosen = jnp.where(octant_col == o, parent_rows, 0.0).astype(BF16)
        lowered += lax.dot_general(
            chosen, shift[o], (((1,), (1,)), ((), ())), preferred_element_type=F32
        )
    far[...] = lowered

    for copy in halo_copies:
        copy.wait()
    leaf_local = far[...] + listed_sum(win, ops, hot, key, picked, lhs)

    own_lanes = iota((harm, coeffs), 1) // harm == iota((harm, coeffs), 0)
    for part_number, value in enumerate(split(leaf_local)):
        value = value.astype(F32)
        for n in range(leaves):
            row = jnp.broadcast_to(value[n : n + 1], (harm, coeffs))
            leaf_rows[part_number, n * harm : (n + 1) * harm, :] = jnp.where(
                own_lanes, row, 0.0
            ).astype(BF16)
    group = box_tile * harm
    main = dot(leaf_rows[0], cboth[...])
    value = main[:, :shell] + main[:, shell:] + dot(leaf_rows[1], cboth[:, :shell])
    high, low = split(value)
    for t in range(tiles):
        rows = slice(t * group, (t + 1) * group)
        lanes = slice(t % 2 * shell, (t % 2 + 1) * shell)
        values[t // 2, :group, lanes] = high[rows]
        values[t // 2, group : 2 * group, lanes] = high[rows]
        values[t // 2, 2 * group :, lanes] = low[rows]
    for t in range(0, tiles, 2):
        both = dot(esix[...], values[t // 2])
        out[t] = (both[:, :shell] + near[t]).astype(out.dtype)
        out[t + 1] = (both[:, shell:] + near[t + 1]).astype(out.dtype)


def body(
    leaf_moments,
    leaf_list,
    leaf_op,
    leaf_parent,
    leaf_octant,
    parent_list,
    parent_op,
    operators,
    shift_up,
    density,
    nearby_coulomb_kernel,
    near_src,
    near_kind,
    near_count,
    eval_rows,
    eval_cols,
):
    n_gx, n_yz = lax.axis_size("gx"), lax.axis_size("yz")
    leaf_side, _, coeffs = leaf_moments.shape
    leaves = leaf_side * leaf_side
    slots = leaf_list.shape[2]
    per_dev, pslots = parent_list.shape[1:]
    column = per_dev * n_yz
    ops_count = operators.shape[0]
    tiles, shell, _ = density.shape
    kinds = nearby_coulomb_kernel.shape[0]
    inputs = (
        leaf_moments.reshape(leaves, coeffs),
        leaf_list.reshape(leaves, slots),
        leaf_op.reshape(leaves, slots),
        leaf_parent,
        leaf_octant,
        parent_list[0],
        parent_op[0],
        operators,
        shift_up,
        density,
        nearby_coulomb_kernel,
        near_src,
        near_kind,
        near_count,
        eval_rows.T,
        eval_cols,
    )
    vmem = pl.BlockSpec(memory_space=pltpu.VMEM)
    hbm = pl.BlockSpec(memory_space=pltpu.HBM)
    dma = pltpu.SemaphoreType.DMA
    return pl.pallas_call(
        functools.partial(kernel, n_gx, n_yz, leaf_side),
        out_shape=jax.ShapeDtypeStruct(density.shape, BF16),
        in_specs=[hbm] * INPUTS,
        out_specs=vmem,
        scratch_shapes=[
            *(
                (pltpu.SMEM if i in (11, 12, 13) else pltpu.VMEM)(value.shape, value.dtype)
                for i, value in enumerate(inputs)
            ),
            pltpu.VMEM((9 * leaves, coeffs), BF16),
            pltpu.VMEM((n_yz, per_dev, pslots), jnp.int32),
            pltpu.VMEM((n_yz, per_dev, pslots), jnp.int32),
            pltpu.VMEM((n_yz, column, coeffs), F32),
            pltpu.VMEM((5 * column, coeffs), BF16),
            pltpu.VMEM((kinds * tiles + 1, shell, shell), F32),
            pltpu.VMEM((tiles, shell, shell), F32),
            pltpu.VMEM((leaves, coeffs), F32),
            pltpu.VMEM((slots * leaves, 9 * leaves), BF16),
            pltpu.VMEM((leaves // GROUP, ops_count * GROUP, slots * GROUP), BF16),
            pltpu.VMEM((slots * leaves, coeffs), BF16),
            pltpu.VMEM((2 * leaves, ops_count * coeffs), BF16),
            pltpu.VMEM((pslots * column, 5 * column), BF16),
            pltpu.VMEM((column // GROUP, ops_count * GROUP, pslots * GROUP), BF16),
            pltpu.VMEM((pslots * column, coeffs), BF16),
            pltpu.VMEM((2 * column, ops_count * coeffs), BF16),
            pltpu.VMEM((shell, 3 * leaves // tiles * eval_rows.shape[1]), BF16),
            pltpu.VMEM((coeffs, 2 * shell), BF16),
            pltpu.VMEM((2, leaves * eval_rows.shape[1], coeffs), BF16),
            pltpu.VMEM((tiles // 2, 3 * leaves // tiles * eval_rows.shape[1], 2 * shell), BF16),
            dma((INPUTS,)),
            dma((8,)),
            dma((8,)),
            dma((2, n_yz - 1)),
            dma((2, n_yz - 1)),
            dma((n_yz - 1,)),
            dma((n_yz - 1,)),
            dma((4,)),
            dma((4,)),
        ],
        compiler_params=pltpu.CompilerParams(
            collective_id=0, has_side_effects=True, vmem_limit_bytes=60 * 2**20
        ),
        name="fmm",
    )(*inputs)


def solution(mesh):
    in_specs = (
        P("gx", "yz", None),
        P("gx", "yz", None),
        P("gx", "yz", None),
        P("gx", "yz"),
        P("gx", "yz"),
        P("gx", "yz", None),
        P("gx", "yz", None),
        P(),
        P(),
        P(("gx", "yz"), None, None),
        P(),
        P(("gx", "yz"), None),
        P(("gx", "yz"), None),
        P(("gx", "yz")),
        P(),
        P(),
    )
    out_specs = P(("gx", "yz"), None, None)
    return jax.shard_map(body, mesh=mesh, in_specs=in_specs, out_specs=out_specs, check_vma=False)
```
